256 devices in a mesh: cx: 8 (over z), cy: 32 (over y, x, core).
Axes of the slice: x: 4, y: 4, z: 8, core: 2. Of those that a mesh axis runs over, the one named last changes fastest.
Arguments:
- points_block: bfloat16 [2048, 64, 256], P(('cx', 'cy')), may hold values from -6 to 6
- leaf_basis: bfloat16 [2048, 64, 256], P(('cx', 'cy')), may hold values from -0.375 to 0.375
- near_blocks: bfloat16 [2048, 4, 256, 256], P(('cx', 'cy')), may hold values from -0.1875 to 0.1875
- near_ids: int32 [2048, 4], P(('cx', 'cy')), may hold values from 0 to 2047, as said below
- local_transfer: bfloat16 [1792, 128, 64], P(('cx', 'cy')), may hold values from -0.5 to 0.5
- far_coupling: bfloat16 [2048, 8, 64, 64], P(('cx', 'cy')), may hold values from -0.25 to 0.25
- far_ids: int32 [2048, 8], P(('cx', 'cy')), may hold values from 0 to 2047, as said below
- upper_transfer: bfloat16 [255, 128, 64], replicated, may hold values from -0.5 to 0.5
- upper_coupling: bfloat16 [255, 64, 64], replicated, may hold values from -0.75 to 0.75
Outputs:
- product: bfloat16 [2048, 64, 256], P(('cx', 'cy'))
The draws below stay inside these ranges and needn't reach their ends.
Inputs may be any that keep to these rules, and one draw needn't show every extreme that they name: `near_ids`: slot 0 of each leaf is the leaf itself; every id names a leaf of the same device or of the two devices before or after it, devices numbered in the order cx then cy. `far_ids`: every id names a leaf of the same device or of the two devices before or after it, devices numbered in the order cx then cy.
All inputs are finite; a program needn't handle non-finite values.
Results may differ from the reference program's by a relative error of at most 0.004.
Values may be sent and summed in bfloat16 or wider, within the bound.
No kernel may reach another device: no remote copies, remote signals or barrier semaphores. Data moves between devices by JAX's collectives and lax.ppermute only.
A program may use at most 128 MiB of HBM per device.

```python
import jax
import jax.numpy as jnp
from jax import lax

LEAF = 256
RANK = 64
COLS = 64
KNEAR = 4
KFAR = 8
LDEV = 8
NLEAF = 2048
N_CX = 8
N_CY = 32


def window_ids(key, count):
    leaves = jnp.arange(NLEAF, dtype=jnp.int32)
    owner = leaves // LDEV
    lowest = jnp.maximum(owner - 2, 0) * LDEV
    highest = jnp.minimum(owner + 3, NLEAF // LDEV) * LDEV
    raw_ids = jax.random.randint(key, (NLEAF, count), 0, 1 << 20, dtype=jnp.int32)
    picked = lowest[:, None] + raw_ids % (highest - lowest)[:, None]
    picked = picked.at[0, count - 1].set(0)
    picked = picked.at[NLEAF - 1, count - 1].set(NLEAF - 1)
    return (picked, leaves)


def draw_near_ids(key, part):
    picked, leaves = window_ids(jax.random.fold_in(key, 11), KNEAR)
    return picked.at[:, 0].set(leaves)


def draw_far_ids(key, part):
    picked, leaves = window_ids(jax.random.fold_in(key, 23), KFAR)
    return picked


def level_of(own_key, shape, split, low, top_value):
    loudness = 1.0
    for axis_at, blocks in split:
        draws = jax.random.uniform(jax.random.fold_in(jax.random.fold_in(own_key, 6), axis_at), (blocks,), jnp.float32, low / len(split), top_value / len(split))
        loudness = loudness * jnp.repeat(jnp.exp(draws), shape[axis_at] // blocks).reshape((-1,) + (1,) * (len(shape) - 1 - axis_at))
    return loudness


def noise(key, shape, deviation, most, split=(), kind=jnp.bfloat16):
    drawn = jax.random.normal(key, shape, jnp.float32) * deviation
    if len(split) > 0:
        drawn = level_of(key, shape, split, -0.22, 0.18) * drawn
    return jnp.clip(drawn, min=-most, max=most).astype(kind)


def setup_inputs(seed: int = 0) -> dict:
    splits = jax.random.split(jax.random.key(seed), 10)
    points_block = noise(splits[0], (NLEAF, COLS, LEAF), 1.0, 6.0, ((0, 256),))
    leaf_basis = noise(splits[1], (NLEAF, RANK, LEAF), LEAF ** -0.5, 0.375, ((0, 256),))
    near_blocks = noise(splits[2], (NLEAF, KNEAR, LEAF, LEAF), (LEAF * KNEAR) ** -0.5, 0.1875, ((0, 256),))
    near_ids = draw_near_ids(jax.random.fold_in(splits[9], 71), 0)
    local_transfer = noise(splits[4], ((LDEV - 1) * N_CX * N_CY, 2 * RANK, RANK), (2 * RANK) ** -0.5, 0.5, ((0, 256),))
    far_coupling = noise(splits[5], (NLEAF, KFAR, RANK, RANK), (RANK * KFAR) ** -0.5, 0.25, ((0, 256),))
    far_ids = draw_far_ids(jax.random.fold_in(splits[9], 71), 0)
    upper_transfer = noise(splits[7], (N_CX * N_CY - 1, 2 * RANK, RANK), (2 * RANK) ** -0.5, 0.5)
    upper_coupling = noise(splits[8], (N_CX * N_CY - 1, RANK, RANK), RANK ** -0.5, 0.75)
    return {"points_block": points_block, "leaf_basis": leaf_basis, "near_blocks": near_blocks, "near_ids": near_ids, "local_transfer": local_transfer, "far_coupling": far_coupling, "far_ids": far_ids, "upper_transfer": upper_transfer, "upper_coupling": upper_coupling}


def up_level(transfer, children):
    count = transfer.shape[0]
    stacked = children.reshape(count, 2 * children.shape[1], children.shape[2])
    return jnp.einsum('nkr,nkc->nrc', transfer, stacked, precision=lax.Precision.HIGHEST)


def down_level(transfer, parents):
    count = transfer.shape[0]
    out_rows = jnp.einsum('nkr,nrc->nkc', transfer, parents, precision=lax.Precision.HIGHEST)
    return out_rows.reshape(2 * count, transfer.shape[2], parents.shape[2])


def upper_tree(roots, upper_transfer, upper_coupling):
    count = roots.shape[0]
    offset = 0
    skeleton = roots
    saved = []
    while count > 1:
        half = count // 2
        transfer = upper_transfer[offset:offset + half].astype(jnp.float32)
        coupling = upper_coupling[offset:offset + half].astype(jnp.float32)
        pairs = skeleton.reshape(half, 2, skeleton.shape[1], skeleton.shape[2])
        to_left = jnp.einsum('nab,nbc->nac', coupling, pairs[:, 1], precision=lax.Precision.HIGHEST)
        to_right = jnp.einsum('nba,nbc->nac', coupling, pairs[:, 0], precision=lax.Precision.HIGHEST)
        terms = jnp.stack([to_left, to_right], 1).reshape(count, skeleton.shape[1], skeleton.shape[2])
        saved.append((transfer, terms))
        skeleton = up_level(transfer, skeleton)
        offset = offset + half
        count = half
    coeffs = jnp.zeros_like(skeleton)
    for transfer, terms in reversed(saved):
        coeffs = down_level(transfer, coeffs) + terms
    return coeffs


def reference(points_block, leaf_basis, near_blocks, near_ids, local_transfer, far_coupling, far_ids, upper_transfer, upper_coupling):
    devices = N_CX * N_CY
    skel_leaf = jnp.einsum('lrp,lcp->lrc', leaf_basis.astype(jnp.float32), points_block.astype(jnp.float32), precision=lax.Precision.HIGHEST)
    skel_half = lax.optimization_barrier(skel_leaf.astype(jnp.bfloat16)).astype(jnp.float32)
    local_all = local_transfer.astype(jnp.float32).reshape(devices, LDEV - 1, 2 * RANK, RANK)
    skeleton = skel_leaf
    offset = 0
    width = LDEV // 2
    local_levels = []
    while width >= 1:
        transfer = local_all[:, offset:offset + width].reshape(devices * width, 2 * RANK, RANK)
        local_levels.append(transfer)
        skeleton = up_level(transfer, skeleton)
        offset = offset + width
        width = width // 2
    coeffs = upper_tree(skeleton, upper_transfer, upper_coupling)
    for transfer in reversed(local_levels):
        coeffs = down_level(transfer, coeffs)

    def per_group(inputs):
        basis, blocks, near_rows, coupling, far_rows, leaf_coeffs = inputs
        far_skel = skel_half[far_rows]
        leafcoef = leaf_coeffs + jnp.einsum('lkab,lkbc->lac', coupling.astype(jnp.float32), far_skel, precision=lax.Precision.HIGHEST)
        coef_half = lax.optimization_barrier(leafcoef.astype(jnp.bfloat16)).astype(jnp.float32)
        far_part = jnp.einsum('lrp,lrc->lcp', basis.astype(jnp.float32), coef_half, precision=lax.Precision.HIGHEST)
        near_cols = points_block[near_rows].astype(jnp.float32)
        near_part = jnp.einsum('lkcq,lkpq->lcp', near_cols, blocks.astype(jnp.float32), precision=lax.Precision.HIGHEST)
        return (far_part + near_part).astype(jnp.bfloat16)

    grouped = (leaf_basis.reshape(devices, LDEV, RANK, LEAF),
               near_blocks.reshape(devices, LDEV, KNEAR, LEAF, LEAF),
               near_ids.reshape(devices, LDEV, KNEAR),
               far_coupling.reshape(devices, LDEV, KFAR, RANK, RANK),
               far_ids.reshape(devices, LDEV, KFAR),
               coeffs.reshape(devices, LDEV, RANK, COLS))
    result = lax.map(per_group, grouped)
    return result.reshape(NLEAF, COLS, LEAF)
```

```python
import jax
import jax.numpy as jnp
from jax import lax
from jax.experimental import pallas as pl
from jax.experimental.pallas import tpu as pltpu
from jax.sharding import PartitionSpec as P

F32 = jnp.float32
BF16 = jnp.bfloat16
AXES = ("cx", "cy")
VM = pl.BlockSpec(memory_space=pltpu.VMEM)
SM = pl.BlockSpec(memory_space=pltpu.SMEM)
HB = pl.BlockSpec(memory_space=pltpu.HBM)
ANY = pl.BlockSpec(memory_space=pl.ANY)
HBM = pltpu.HBM
VMEM = pltpu.VMEM


def position():
    return lax.axis_index("cx") * lax.axis_size("cy") + lax.axis_index("cy")


def mm(a, b):
    return lax.dot_general(a, b, (((1,), (0,)), ((), ())), preferred_element_type=F32)


def mt(a, b):
    return lax.dot_general(a, b, (((1,), (1,)), ((), ())), preferred_element_type=F32)


def high_low(x):
    high = x.astype(BF16)
    return high, (x - high.astype(F32)).astype(BF16)


def split(x):
    return jnp.concatenate(high_low(x), axis=0)


def fold(y):
    half = y.shape[0] // 2
    return y[:half] + y[half:]


def up(left, right, transfer):
    return fold(mt(jnp.concatenate([left, right], axis=1), transfer))


def packed(x):
    return jnp.concatenate([x[:32], x[32:]], axis=1)


def unpacked(x):
    return jnp.concatenate([x[:, :64], x[:, 64:]], axis=0)


def leaf_up_kernel(
    points, basis, local, transfer, halo, root_out, first_out, plane_out, basis_here, local_here, sems
):
    pos = position()
    plane = pos >> 5
    copies = [
        (points, halo.at[pl.ds(0, 8)]), (basis, basis_here), (local, local_here),
        (transfer.at[pos >> 1], first_out),
    ]
    base = 128
    at = 0
    for count in (8, 4, 2, 1):
        copies.append((transfer.at[pl.ds(base + plane * count, count)], plane_out.at[pl.ds(at, count)]))
        base += count * 8
        at += count
    handles = [pltpu.make_async_copy(a, b, sems.at[i]) for i, (a, b) in enumerate(copies)]
    for handle in handles:
        handle.start()
    for handle in handles[:2]:
        handle.wait()
    skel = [mt(halo[g], basis_here[g]) for g in range(8)]
    handles[2].wait()
    for half in range(2):
        halo[8 + half] = jnp.concatenate(skel[4 * half : 4 * half + 4], axis=1).astype(BF16)
    offset = 0
    while len(skel) > 1:
        parts = [split(x) for x in skel]
        skel = [
            up(parts[2 * n], parts[2 * n + 1], local_here[offset + n])
            for n in range(len(parts) // 2)
        ]
        offset += len(skel)
    root_out[...] = packed(skel[0])
    for handle in handles[3:]:
        handle.wait()


def merge_kernel(root, partner, transfer, message, sibling):
    odd = position() & 1
    own = unpacked(root[...])
    other = unpacked(partner[...])
    sibling[...] = other
    left = split(jnp.where(odd == 1, other, own))
    right = split(jnp.where(odd == 1, own, other))
    merged = packed(up(left, right, transfer[...]))
    for peer in range(16):
        message[peer] = merged


def assemble_kernel(halo, partner, pair, sems):
    odd = position() & 1
    handles = [
        pltpu.make_async_copy(halo, pair.at[odd], sems.at[0]),
        pltpu.make_async_copy(partner, pair.at[1 - odd], sems.at[1]),
    ]
    for handle in handles:
        handle.start()
    for handle in handles:
        handle.wait()


def halves_of(x):
    return x[:, :64], x[:, 64:]


def weights_kernel(
    transfer, coupling_in, local_in, basis, blocks, far_coupling,
    top_out, down_high, down_low, leaf_high, leaf_low, basis_out, blocks_out, far_coupling_out,
    own_transfer, own_coupling, coupling, local, sems,
):
    pos = position()
    copies = [(coupling_in, coupling), (local_in, local)]
    base = 0
    for level in range(1, 9):
        copies.append((transfer.at[base + (pos >> level)], own_transfer.at[level - 1]))
        base += 256 >> level
    early = len(copies)
    copies += [
        (transfer.at[pl.ds(248, 6)], top_out), (far_coupling, far_coupling_out),
        (basis, basis_out), (blocks, blocks_out),
    ]
    handles = [pltpu.make_async_copy(a, b, sems.at[i]) for i, (a, b) in enumerate(copies)]
    for handle in handles:
        handle.start()
    for handle in handles[:early]:
        handle.wait()
    level_of_row = lax.broadcasted_iota(jnp.int32, (8, 255), 0) + 1
    wanted = 256 - (512 >> level_of_row) + (pos >> level_of_row)
    pick = jnp.where(lax.broadcasted_iota(jnp.int32, (8, 255), 1) == wanted, 1.0, 0.0).astype(BF16)
    for row in range(64):
        own_coupling[row] = mt(pick, coupling[row])
    tops = list(halves_of(local[6].astype(F32)))
    for first, count in ((4, 2), (0, 4)):
        products = []
        for n in range(count):
            products.append(fold(mm(split(tops[n]), local[first + n])))
        if first:
            tops = [half for x in products for half in halves_of(x)]
    for n in range(4):
        leaf_high[n], leaf_low[n] = high_low(products[n])
    row = lax.broadcasted_iota(jnp.int32, (64, 64), 0)
    col = lax.broadcasted_iota(jnp.int32, (64, 64), 1)
    path = jnp.where(row == col, 1.0, 0.0).astype(F32)
    for level in range(1, 9):
        side = (pos >> (level - 1)) & 1
        both = split(path)
        block = own_coupling[:, level - 1, :].astype(BF16)
        term = jnp.where(side == 0, fold(mm(both, block)), fold(mt(both, block)))
        down_high[level - 1], down_low[level - 1] = high_low(term)
        if level < 8:
            left, right = halves_of(own_transfer[level - 1])
            path = fold(mt(both, jnp.where(side == 0, left, right)))
    for handle in handles[early:]:
        handle.wait()


def sweep(first, transfer, nodes, levels):
    parts = first
    offset = 0
    at = 0
    for _ in range(levels):
        count = len(parts) // 2
        halves = [split(x) for x in parts]
        parts = [
            up(halves[2 * n], halves[2 * n + 1], transfer[offset + n]) for n in range(count)
        ]
        offset += count
        at += 2 * count
        for n in range(count):
            nodes[at + n] = parts[n]
    return parts


def plane_kernel(received, transfer, message, siblings, nodes):
    first = [unpacked(received[n]) for n in range(16)]
    for n in range(16):
        nodes[n] = first[n]
    top = sweep(first, transfer, nodes, 4)
    root = packed(top[0])
    for peer in range(8):
        message[peer] = root
    own = (position() >> 1) & 15
    at = 0
    for level in range(4):
        siblings[level] = nodes[at + ((own >> level) ^ 1)]
        at += 16 >> level


def add_terms(total, siblings, down_high, down_low, first):
    for n, sibling in enumerate(siblings):
        both = split(sibling)
        total = total + fold(mt(both, down_high[first + n])) + mt(both[:64], down_low[first + n])
    return total


def near_far_kernel(
    near_ids, far_ids, pair, moved, passed, blocks, coupling, sibling, siblings,
    down_high, down_low, near_out, far_out, coef_out, skels,
):
    pos = position()
    odd = pos & 1
    pair_at, moved_at, passed_at = 2 - odd, 3 * odd, 4 - 4 * odd
    coef_out[...] = add_terms(
        jnp.zeros((64, 64), F32), [sibling[...]] + [siblings[n] for n in range(4)],
        down_high, down_low, 0,
    )
    first_leaf = (pos - 2) * 8
    for source, at, count in ((pair, pair_at, 2), (moved, moved_at, 2), (passed, passed_at, 1)):
        for device in range(count):
            for leaf in range(8):
                lane = 64 * (leaf % 4)
                skels[8 * (at + device) + leaf] = source[device, 8 + leaf // 4, :, lane : lane + 64]
    for g in range(8):
        total = mt(pair[odd, g], blocks[g, 0])
        for k in range(1, 4):
            place = jnp.clip(near_ids[k, g] - first_leaf, 0, 39)
            device, leaf = place >> 3, place & 7
            from_pair, from_moved = device - pair_at, device - moved_at
            cols = jnp.where(
                (from_pair >> 1) == 0, pair[from_pair & 1, leaf],
                jnp.where(
                    (from_moved >> 1) == 0, moved[from_moved & 1, leaf], passed[0, leaf]
                ),
            )
            total = total + mt(cols, blocks[g, k])
        near_out[g] = total
        total = None
        for k in range(8):
            place = jnp.clip(far_ids[g, k] - first_leaf, 0, 39)
            term = mt(skels[place], coupling[g, k])
            total = term if total is None else total + term
        far_out[g] = total


def final_kernel(
    received, transfer, down_high, down_low, leaf_high, leaf_low, coef, near, far, basis, out, nodes,
):
    first = [unpacked(received[n]) for n in range(8)]
    for n in range(8):
        nodes[n] = first[n]
    sweep(first, transfer, nodes, 2)
    own = position() >> 5
    siblings = []
    at = 0
    for level in range(3):
        siblings.append(nodes[at + ((own >> level) ^ 1)])
        at += 8 >> level
    total = add_terms(coef[...], siblings, down_high, down_low, 5)
    both = split(total)
    for pair in range(4):
        coefs = fold(mm(both, leaf_high[pair])) + mm(both[:64], leaf_low[pair])
        for side, part in enumerate(halves_of(coefs)):
            g = 2 * pair + side
            half = (part + far[g]).astype(BF16)
            out[g] = (mm(half, basis[g]) + near[g]).astype(BF16)


def call(kernel, ins, outs, in_specs, scratch=(), limit=4, out_spec=VM):
    ins = [
        pltpu.with_memory_space_constraint(x, pltpu.HBM) if spec is HB else x
        for x, spec in zip(ins, in_specs)
    ]
    return pl.pallas_call(
        kernel,
        out_shape=[space(shape, dtype) for shape, dtype, space in outs],
        in_specs=in_specs,
        out_specs=[out_spec] * len(outs),
        scratch_shapes=list(scratch),
        compiler_params=pltpu.CompilerParams(vmem_limit_bytes=limit << 20),
    )(*ins)


def groups_of(bits):
    mask = sum(1 << b for b in bits)
    found = {}
    for device in range(256):
        found.setdefault(device & ~mask, []).append(device)
    return list(found.values())


def exchange(message, bits):
    return lax.all_to_all(message, AXES, 0, 0, axis_index_groups=groups_of(bits))


def swapped(value):
    return lax.ppermute(value, AXES, [(i, i ^ 1) for i in range(lax.axis_size(AXES))])


def outward(value):
    count = lax.axis_size(AXES)
    pairs = [(i, i + 2 - 4 * (i % 2)) for i in range(count)]
    return lax.ppermute(value, AXES, [(i, j) for i, j in pairs if 0 <= j < count])


def local(
    points, basis, near_blocks, near_ids, local_transfer, far_coupling, far_ids,
    upper_transfer, upper_coupling,
):
    near_ids = near_ids.T
    local_transfer = jnp.swapaxes(local_transfer, 1, 2)
    upper_transfer = jnp.swapaxes(upper_transfer, 1, 2)
    upper_coupling = jnp.transpose(upper_coupling, (1, 2, 0))
    halo, root, first, plane = call(
        leaf_up_kernel, (points, basis, local_transfer, upper_transfer),
        [
            ((10, 64, 256), BF16, HBM), ((32, 128), F32, VMEM), ((64, 128), BF16, VMEM),
            ((15, 64, 128), BF16, VMEM),
        ],
        [HB] * 4,
        [pltpu.VMEM((8, 64, 256), BF16), pltpu.VMEM((7, 64, 128), BF16), pltpu.SemaphoreType.DMA((8,))],
    )
    partner = swapped(root)
    partner_halo = swapped(halo)
    message, sibling = call(
        merge_kernel, (root, partner, first),
        [((16, 32, 128), F32, HBM), ((64, 64), F32, VMEM)], [VM] * 3,
    )
    received = exchange(message, (1, 2, 3, 4))
    (pair,) = call(
        assemble_kernel, (halo, partner_halo), [((2, 10, 64, 256), BF16, VMEM)],
        [HB, ANY], [pltpu.SemaphoreType.DMA((2,))],
    )
    moved = outward(pair)
    message, siblings = call(
        plane_kernel, (received, plane),
        [((8, 32, 128), F32, HBM), ((4, 64, 64), F32, VMEM)], [VM] * 2,
        [pltpu.VMEM((31, 64, 64), F32)],
    )
    received = exchange(message, (5, 6, 7))
    odd = lax.axis_index("cy") & 1
    passed = swapped(lax.dynamic_slice_in_dim(moved, 1 - odd, 1, 0))
    top, down_high, down_low, leaf_high, leaf_low, basis, near_blocks, far_coupling = call(
        weights_kernel,
        (upper_transfer, upper_coupling, local_transfer, basis, near_blocks, far_coupling),
        [((6, 64, 128), BF16, VMEM)] + [((8, 64, 64), BF16, VMEM)] * 2
        + [((4, 64, 128), BF16, VMEM)] * 2
        + [((8, 64, 256), BF16, VMEM), ((8, 4, 256, 256), BF16, VMEM), ((8, 8, 64, 64), BF16, VMEM)],
        [HB] * 6,
        [
            pltpu.VMEM((8, 64, 128), BF16), pltpu.VMEM((64, 8, 64), F32),
            pltpu.VMEM((64, 64, 255), BF16), pltpu.VMEM((7, 64, 128), BF16),
            pltpu.SemaphoreType.DMA((14,)),
        ],
        limit=8,
    )
    near, far, coef = call(
        near_far_kernel,
        (near_ids, far_ids, pair, moved, passed, near_blocks, far_coupling, sibling, siblings,
         down_high, down_low),
        [((8, 64, 256), F32, VMEM), ((8, 64, 64), F32, VMEM), ((64, 64), F32, VMEM)],
        [SM, SM] + [VM] * 9,
        [pltpu.VMEM((40, 64, 64), BF16)],
    )
    (out,) = call(
        final_kernel,
        (received, top, down_high, down_low, leaf_high, leaf_low, coef, near, far, basis),
        [((8, 64, 256), BF16, HBM)], [VM] * 10,
        [pltpu.VMEM((14, 64, 64), F32)],
    )
    return out


def solution(mesh):
    return jax.shard_map(
        local,
        mesh=mesh,
        in_specs=(
            P(AXES, None, None),
            P(AXES, None, None),
            P(AXES, None, None, None),
            P(AXES, None),
            P(AXES, None, None),
            P(AXES, None, None, None),
            P(AXES, None),
            P(),
            P(),
        ),
        out_specs=P(AXES, None, None),
        check_vma=False,
    )
```

```python
import jax
import jax.numpy as jnp
from jax import lax
from jax.experimental import pallas as pl
from jax.experimental.pallas import tpu as pltpu
from jax.sharding import PartitionSpec as P

F32 = jnp.float32
BF16 = jnp.bfloat16
AXES = ("cx", "cy")
VM = pl.BlockSpec(memory_space=pltpu.VMEM)
SM = pl.BlockSpec(memory_space=pltpu.SMEM)
HB = pl.BlockSpec(memory_space=pltpu.HBM)
ANY = pl.BlockSpec(memory_space=pl.ANY)
HBM = pltpu.HBM
VMEM = pltpu.VMEM


def position():
    return lax.axis_index("cx") * lax.axis_size("cy") + lax.axis_index("cy")


def mm(a, b):
    return lax.dot_general(a, b, (((1,), (0,)), ((), ())), preferred_element_type=F32)


def mt(a, b):
    return lax.dot_general(a, b, (((1,), (1,)), ((), ())), preferred_element_type=F32)


def high_low(x):
    high = x.astype(BF16)
    return high, (x - high.astype(F32)).astype(BF16)


def split(x):
    return jnp.concatenate(high_low(x), axis=0)


def fold(y):
    half = y.shape[0] // 2
    return y[:half] + y[half:]


def paired(left, right):
    return jnp.concatenate([left, right], axis=1)


def up(pair, transfer):
    return fold(mt(split(pair), transfer))


def packed(x):
    return jnp.concatenate([x[:32], x[32:]], axis=1)


def unpacked(x):
    return jnp.concatenate([x[:, :64], x[:, 64:]], axis=0)


def leaf_up_kernel(
    points, basis, local, transfer, halo, root_out, first_out, plane_out, basis_here, local_here, sems
):
    pos = position()
    plane = pos >> 5
    copies = [
        (points, halo.at[pl.ds(0, 8)]), (basis, basis_here), (local, local_here),
        (transfer.at[pos >> 1], first_out),
    ]
    base = 128
    at = 0
    for count in (8, 4, 2, 1):
        copies.append((transfer.at[pl.ds(base + plane * count, count)], plane_out.at[pl.ds(at, count)]))
        base += count * 8
        at += count
    handles = [pltpu.make_async_copy(a, b, sems.at[i]) for i, (a, b) in enumerate(copies)]
    for handle in handles:
        handle.start()
    for handle in handles[:2]:
        handle.wait()
    skel = [mt(halo[g], basis_here[g]) for g in range(8)]
    pairs = [paired(skel[2 * n], skel[2 * n + 1]) for n in range(4)]
    for half in range(2):
        halo[8 + half] = paired(pairs[2 * half], pairs[2 * half + 1]).astype(BF16)
    handles[2].wait()
    offset = 0
    while True:
        skel = [up(pair, local_here[offset + n]) for n, pair in enumerate(pairs)]
        if len(skel) == 1:
            break
        offset += len(skel)
        pairs = [paired(skel[2 * n], skel[2 * n + 1]) for n in range(len(skel) // 2)]
    root_out[...] = packed(skel[0])
    for handle in handles[3:]:
        handle.wait()


def merge_kernel(root, partner, transfer, message, sibling):
    odd = position() & 1
    own = unpacked(root[...])
    other = unpacked(partner[...])
    sibling[...] = other
    pair = jnp.where(odd == 1, paired(other, own), paired(own, other))
    merged = packed(up(pair, transfer[...]))
    for peer in range(16):
        message[peer] = merged


def assemble_kernel(halo, partner, pair, sems):
    odd = position() & 1
    handles = [
        pltpu.make_async_copy(halo, pair.at[odd], sems.at[0]),
        pltpu.make_async_copy(partner, pair.at[1 - odd], sems.at[1]),
    ]
    for handle in handles:
        handle.start()
    for handle in handles:
        handle.wait()


def halves_of(x):
    return x[:, :64], x[:, 64:]


def weights_kernel(
    transfer, coupling_in, local_in, basis, blocks, far_coupling,
    cross_high, cross_low, down_high, down_low, leaf_high, leaf_low, basis_out, blocks_out,
    far_coupling_out, top, own_transfer, own_coupling, coupling, local, sems,
):
    pos = position()
    copies = [(coupling_in, coupling), (local_in, local)]
    base = 0
    for level in range(1, 9):
        copies.append((transfer.at[base + (pos >> level)], own_transfer.at[level - 1]))
        base += 256 >> level
    early = len(copies)
    copies += [
        (transfer.at[pl.ds(248, 6)], top), (far_coupling, far_coupling_out),
        (basis, basis_out), (blocks, blocks_out),
    ]
    handles = [pltpu.make_async_copy(a, b, sems.at[i]) for i, (a, b) in enumerate(copies)]
    for handle in handles:
        handle.start()
    for handle in handles[:early]:
        handle.wait()
    level_of_row = lax.broadcasted_iota(jnp.int32, (8, 255), 0) + 1
    wanted = 256 - (512 >> level_of_row) + (pos >> level_of_row)
    pick = jnp.where(lax.broadcasted_iota(jnp.int32, (8, 255), 1) == wanted, 1.0, 0.0).astype(BF16)
    for row in range(16):
        found = mt(pick, coupling[4 * row : 4 * row + 4].reshape(256, 255))
        for part in range(4):
            own_coupling[4 * row + part] = found[:, 64 * part : 64 * part + 64]
    tops = list(halves_of(local[6].astype(F32)))
    for first, count in ((4, 2), (0, 4)):
        products = []
        for n in range(count):
            products.append(fold(mm(split(tops[n]), local[first + n])))
        if first:
            tops = [half for x in products for half in halves_of(x)]
    for n in range(4):
        leaf_high[n], leaf_low[n] = high_low(products[n])
    row = lax.broadcasted_iota(jnp.int32, (64, 64), 0)
    col = lax.broadcasted_iota(jnp.int32, (64, 64), 1)
    path = jnp.where(row == col, 1.0, 0.0).astype(F32)
    terms = []
    for level in range(1, 9):
        side = (pos >> (level - 1)) & 1
        both = split(path)
        block = own_coupling[:, level - 1, :].astype(BF16)
        term = jnp.where(side == 0, fold(mm(both, block)), fold(mt(both, block)))
        down_high[level - 1], down_low[level - 1] = high_low(term)
        terms.append(term)
        if level < 8:
            left, right = halves_of(own_transfer[level - 1])
            path = fold(mt(both, jnp.where(side == 0, left, right)))
    plane = pos >> 5
    handles[early].wait()
    near_node = (plane >> 1) ^ 1
    far_node = (plane >> 2) ^ 1
    two = fold(mm(split(terms[6]), top[near_node]))
    halves = halves_of(fold(mm(split(terms[7]), top[4 + far_node])))
    fours = [fold(mm(split(half), top[2 * far_node + n])) for n, half in enumerate(halves)]
    for n, wide in enumerate([two] + fours):
        cross_high[n], cross_low[n] = high_low(wide)
    for handle in handles[early + 1 :]:
        handle.wait()


def unpacked_pair(left, right):
    top = jnp.concatenate([left[:, :64], right[:, :64]], axis=1)
    bottom = jnp.concatenate([left[:, 64:], right[:, 64:]], axis=1)
    return jnp.concatenate([top, bottom], axis=0)


def plane_kernel(received, transfer, message, siblings, nodes):
    pairs = [unpacked_pair(received[2 * n], received[2 * n + 1]) for n in range(8)]
    offset = 0
    while True:
        tops = [up(pair, transfer[offset + n]) for n, pair in enumerate(pairs)]
        if len(tops) == 1:
            break
        for n, top in enumerate(tops):
            nodes[offset + n] = top
        offset += len(tops)
        pairs = [paired(tops[2 * n], tops[2 * n + 1]) for n in range(len(tops) // 2)]
    root = packed(tops[0])
    for peer in range(8):
        message[peer] = root
    own = (position() >> 1) & 15
    siblings[0] = unpacked(received[own ^ 1])
    siblings[1] = nodes[(own >> 1) ^ 1]
    siblings[2] = nodes[8 + ((own >> 2) ^ 1)]
    siblings[3] = nodes[12 + ((own >> 3) ^ 1)]


def add_terms(total, siblings, down_high, down_low, first):
    for n, sibling in enumerate(siblings):
        both = split(sibling)
        total = total + fold(mt(both, down_high[first + n])) + mt(both[:64], down_low[first + n])
    return total


def near_far_kernel(
    near_ids, far_ids, pair, moved, passed, blocks, coupling, sibling, siblings,
    down_high, down_low, near_out, far_out, coef_out, skels,
):
    pos = position()
    odd = pos & 1
    pair_at, moved_at, passed_at = 2 - odd, 3 * odd, 4 - 4 * odd
    coef_out[...] = add_terms(
        jnp.zeros((64, 64), F32), [sibling[...]] + [siblings[n] for n in range(4)],
        down_high, down_low, 0,
    )
    first_leaf = (pos - 2) * 8
    for source, at, count in ((pair, pair_at, 2), (moved, moved_at, 2), (passed, passed_at, 1)):
        for device in range(count):
            for leaf in range(8):
                lane = 64 * (leaf % 4)
                skels[8 * (at + device) + leaf] = source[device, 8 + leaf // 4, :, lane : lane + 64]
    for g in range(8):
        total = mt(pair[odd, g], blocks[g, 0])
        for k in range(1, 4):
            place = jnp.clip(near_ids[k, g] - first_leaf, 0, 39)
            device, leaf = place >> 3, place & 7
            from_pair, from_moved = device - pair_at, device - moved_at
            cols = jnp.where(
                (from_pair >> 1) == 0, pair[from_pair & 1, leaf],
                jnp.where(
                    (from_moved >> 1) == 0, moved[from_moved & 1, leaf], passed[0, leaf]
                ),
            )
            total = total + mt(cols, blocks[g, k])
        near_out[g] = total
        total = None
        for k in range(8):
            place = jnp.clip(far_ids[g, k] - first_leaf, 0, 39)
            term = mt(skels[place], coupling[g, k])
            total = term if total is None else total + term
        far_out[g] = total


def final_kernel(
    received, cross_high, cross_low, down_high, down_low, leaf_high, leaf_low, coef, near, far, basis,
    out,
):
    own = position() >> 5
    two = ((own >> 1) ^ 1) * 2
    four = ((own >> 2) ^ 1) * 4
    total = add_terms(coef[...], [unpacked(received[own ^ 1])], down_high, down_low, 5)
    for n, first in enumerate((two, four, four + 2)):
        both = split(unpacked_pair(received[first], received[first + 1]))
        total = total + fold(mt(both, cross_high[n])) + mt(both[:64], cross_low[n])
    both = split(total)
    for pair in range(4):
        coefs = fold(mm(both, leaf_high[pair])) + mm(both[:64], leaf_low[pair])
        for side, part in enumerate(halves_of(coefs)):
            g = 2 * pair + side
            half = (part + far[g]).astype(BF16)
            out[g] = (mm(half, basis[g]) + near[g]).astype(BF16)


def call(kernel, ins, outs, in_specs, scratch=(), limit=4, out_spec=VM):
    ins = [
        pltpu.with_memory_space_constraint(x, pltpu.HBM) if spec is HB else x
        for x, spec in zip(ins, in_specs)
    ]
    return pl.pallas_call(
        kernel,
        out_shape=[space(shape, dtype) for shape, dtype, space in outs],
        in_specs=in_specs,
        out_specs=[out_spec] * len(outs),
        scratch_shapes=list(scratch),
        compiler_params=pltpu.CompilerParams(vmem_limit_bytes=limit << 20),
    )(*ins)


def groups_of(bits):
    mask = sum(1 << b for b in bits)
    found = {}
    for device in range(256):
        found.setdefault(device & ~mask, []).append(device)
    return list(found.values())


def exchange(message, bits):
    return lax.all_to_all(message, AXES, 0, 0, axis_index_groups=groups_of(bits))


def swapped(value):
    return lax.ppermute(value, AXES, [(i, i ^ 1) for i in range(lax.axis_size(AXES))])


def outward(value):
    count = lax.axis_size(AXES)
    pairs = [(i, i + 2 - 4 * (i % 2)) for i in range(count)]
    return lax.ppermute(value, AXES, [(i, j) for i, j in pairs if 0 <= j < count])


def local(
    points, basis, near_blocks, near_ids, local_transfer, far_coupling, far_ids,
    upper_transfer, upper_coupling,
):
    near_ids = near_ids.T
    local_transfer = jnp.swapaxes(local_transfer, 1, 2)
    upper_transfer = jnp.swapaxes(upper_transfer, 1, 2)
    upper_coupling = jnp.transpose(upper_coupling, (1, 2, 0))
    halo, root, first, plane = call(
        leaf_up_kernel, (points, basis, local_transfer, upper_transfer),
        [
            ((10, 64, 256), BF16, VMEM), ((32, 128), F32, VMEM), ((64, 128), BF16, VMEM),
            ((15, 64, 128), BF16, VMEM),
        ],
        [HB] * 4,
        [pltpu.VMEM((8, 64, 256), BF16), pltpu.VMEM((7, 64, 128), BF16), pltpu.SemaphoreType.DMA((8,))],
    )
    partner = swapped(root)
    partner_halo = swapped(halo)
    message, sibling = call(
        merge_kernel, (root, partner, first),
        [((16, 32, 128), F32, HBM), ((64, 64), F32, VMEM)], [VM] * 3,
    )
    received = exchange(message, (1, 2, 3, 4))
    (pair,) = call(
        assemble_kernel, (halo, partner_halo), [((2, 10, 64, 256), BF16, VMEM)],
        [ANY, ANY], [pltpu.SemaphoreType.DMA((2,))],
    )
    moved = outward(pair)
    message, siblings = call(
        plane_kernel, (received, plane),
        [((8, 32, 128), F32, HBM), ((4, 64, 64), F32, VMEM)], [VM] * 2,
        [pltpu.VMEM((14, 64, 64), F32)],
    )
    received = exchange(message, (5, 6, 7))
    odd = lax.axis_index("cy") & 1
    passed = swapped(lax.dynamic_slice_in_dim(moved, 1 - odd, 1, 0))
    (
        cross_high, cross_low, down_high, down_low, leaf_high, leaf_low, basis, near_blocks,
        far_coupling,
    ) = call(
        weights_kernel,
        (upper_transfer, upper_coupling, local_transfer, basis, near_blocks, far_coupling),
        [((3, 64, 128), BF16, VMEM)] * 2 + [((8, 64, 64), BF16, VMEM)] * 2
        + [((4, 64, 128), BF16, VMEM)] * 2
        + [((8, 64, 256), BF16, VMEM), ((8, 4, 256, 256), BF16, VMEM), ((8, 8, 64, 64), BF16, VMEM)],
        [HB] * 6,
        [
            pltpu.VMEM((6, 64, 128), BF16), pltpu.VMEM((8, 64, 128), BF16),
            pltpu.VMEM((64, 8, 64), F32),
            pltpu.VMEM((64, 64, 255), BF16), pltpu.VMEM((7, 64, 128), BF16),
            pltpu.SemaphoreType.DMA((14,)),
        ],
        limit=8,
    )
    near, far, coef = call(
        near_far_kernel,
        (near_ids, far_ids, pair, moved, passed, near_blocks, far_coupling, sibling, siblings,
         down_high, down_low),
        [((8, 64, 256), F32, VMEM), ((8, 64, 64), F32, VMEM), ((64, 64), F32, VMEM)],
        [SM, SM] + [VM] * 9,
        [pltpu.VMEM((40, 64, 64), BF16)],
    )
    (out,) = call(
        final_kernel,
        (received, cross_high, cross_low, down_high, down_low, leaf_high, leaf_low, coef, near, far, basis),
        [((8, 64, 256), BF16, HBM)], [VM] * 11,
    )
    return out


def solution(mesh):
    return jax.shard_map(
        local,
        mesh=mesh,
        in_specs=(
            P(AXES, None, None),
            P(AXES, None, None),
            P(AXES, None, None, None),
            P(AXES, None),
            P(AXES, None, None),
            P(AXES, None, None, None),
            P(AXES, None),
            P(),
            P(),
        ),
        out_specs=P(AXES, None, None),
        check_vma=False,
    )
```

```python
import jax
import jax.numpy as jnp
from jax import lax
from jax.experimental import pallas as pl
from jax.experimental.pallas import tpu as pltpu
from jax.sharding import PartitionSpec as P

F32 = jnp.float32
BF16 = jnp.bfloat16
AXES = ("cx", "cy")
VM = pl.BlockSpec(memory_space=pltpu.VMEM)
SM = pl.BlockSpec(memory_space=pltpu.SMEM)
HB = pl.BlockSpec(memory_space=pltpu.HBM)
ANY = pl.BlockSpec(memory_space=pl.ANY)
HBM = pltpu.HBM
VMEM = pltpu.VMEM


def position():
    return lax.axis_index("cx") * lax.axis_size("cy") + lax.axis_index("cy")


def mm(a, b):
    return lax.dot_general(a, b, (((1,), (0,)), ((), ())), preferred_element_type=F32)


def mt(a, b):
    return lax.dot_general(a, b, (((1,), (1,)), ((), ())), preferred_element_type=F32)


def high_low(x):
    high = x.astype(BF16)
    return high, (x - high.astype(F32)).astype(BF16)


def split(x):
    return jnp.concatenate(high_low(x), axis=0)


def fold(y):
    half = y.shape[0] // 2
    return y[:half] + y[half:]


def halves_of(x):
    return x[:, :64], x[:, 64:]


def paired(left, right):
    return jnp.concatenate([left, right], axis=1)


def up(left, right, transfer):
    return fold(mt(split(left), transfer[0]) + mt(split(right), transfer[1]))


def up_packed(left, right, wide):
    return fold(mt(split(paired(left, right)), wide))


def widened(transfer):
    low = (lax.broadcasted_iota(jnp.int32, (64, 128), 1) < 64).astype(F32).astype(BF16)
    high = (lax.broadcasted_iota(jnp.int32, (64, 128), 1) >= 64).astype(F32).astype(BF16)
    turned = jnp.concatenate([transfer[:, 64:], transfer[:, :64]], axis=1)
    top = paired(transfer * low, turned * low)
    bottom = paired(turned * high, transfer * high)
    return jnp.concatenate([top, bottom], axis=0)


def packed(x):
    return jnp.concatenate([x[:32], x[32:]], axis=1)


def unpacked(x):
    return jnp.concatenate([x[:, :64], x[:, 64:]], axis=0)


def leaf_up_kernel(
    points, basis, local, transfer, halo, root_out, first_out, plane_out, basis_here, local_here,
    first_here, sems,
):
    pos = position()
    plane = pos >> 5
    copies = [
        (points, halo.at[pl.ds(0, 8)]), (basis, basis_here), (local, local_here),
        (transfer.at[pos >> 1], first_here),
    ]
    base = 128
    at = 0
    for count in (8, 4, 2, 1):
        copies.append((transfer.at[pl.ds(base + plane * count, count)], plane_out.at[pl.ds(at, count)]))
        base += count * 8
        at += count
    handles = [pltpu.make_async_copy(a, b, sems.at[i]) for i, (a, b) in enumerate(copies)]
    for handle in handles:
        handle.start()
    for handle in handles[:2]:
        handle.wait()
    skel = [mt(halo[g], basis_here[g]) for g in range(8)]
    for half in range(2):
        halo[8 + half] = jnp.concatenate(skel[4 * half : 4 * half + 4], axis=1).astype(BF16)
    handles[2].wait()
    offset = 0
    while len(skel) > 1:
        skel = [
            up(skel[2 * n], skel[2 * n + 1], halves_of(local_here[offset + n]))
            for n in range(len(skel) // 2)
        ]
        offset += len(skel)
    root_out[...] = skel[0]
    handles[3].wait()
    first_out[0], first_out[1] = halves_of(first_here[...])
    for handle in handles[4:]:
        handle.wait()


def merge_kernel(root, partner, transfer, message, sibling):
    odd = position() & 1
    own = root[...]
    other = partner[...]
    sibling[...] = other
    left = jnp.where(odd == 1, other, own)
    right = jnp.where(odd == 1, own, other)
    merged = packed(up(left, right, (transfer[0], transfer[1]))).astype(BF16)
    for peer in range(16):
        message[peer] = merged


def assemble_kernel(halo, partner, pair, sems):
    odd = position() & 1
    handles = [
        pltpu.make_async_copy(halo, pair.at[odd], sems.at[0]),
        pltpu.make_async_copy(partner, pair.at[1 - odd], sems.at[1]),
    ]
    for handle in handles:
        handle.start()
    for handle in handles:
        handle.wait()


def weights_kernel(
    transfer, coupling_in, local_in, basis, blocks, far_coupling,
    next_high, next_low, cross_high, cross_low, down_high, down_low, leaf_high, leaf_low, basis_out,
    blocks_out, far_coupling_out, top, own_transfer, own_coupling, coupling, local, sems,
):
    pos = position()
    copies = [(coupling_in, coupling), (local_in, local)]
    base = 0
    for level in range(1, 9):
        copies.append((transfer.at[base + (pos >> level)], own_transfer.at[level - 1]))
        base += 256 >> level
    early = len(copies)
    copies += [
        (transfer.at[pl.ds(248, 6)], top), (far_coupling, far_coupling_out),
        (basis, basis_out), (blocks, blocks_out),
    ]
    handles = [pltpu.make_async_copy(a, b, sems.at[i]) for i, (a, b) in enumerate(copies)]
    for handle in handles:
        handle.start()
    for handle in handles[:early]:
        handle.wait()
    level_of_row = lax.broadcasted_iota(jnp.int32, (8, 255), 0) + 1
    wanted = 256 - (512 >> level_of_row) + (pos >> level_of_row)
    pick = jnp.where(lax.broadcasted_iota(jnp.int32, (8, 255), 1) == wanted, 1.0, 0.0).astype(BF16)
    for row in range(16):
        found = mt(pick, coupling[4 * row : 4 * row + 4].reshape(256, 255))
        for part in range(4):
            own_coupling[4 * row + part] = found[:, 64 * part : 64 * part + 64]
    tops = list(halves_of(local[6].astype(F32)))
    for first, count in ((4, 2), (0, 4)):
        products = []
        for n in range(count):
            products.append(fold(mm(split(tops[n]), local[first + n])))
        if first:
            tops = [half for x in products for half in halves_of(x)]
    for n in range(4):
        leaf_high[n], leaf_low[n] = high_low(products[n])
    row = lax.broadcasted_iota(jnp.int32, (64, 64), 0)
    col = lax.broadcasted_iota(jnp.int32, (64, 64), 1)
    path = jnp.where(row == col, 1.0, 0.0).astype(F32)
    terms = []
    for level in range(1, 9):
        side = (pos >> (level - 1)) & 1
        both = split(path)
        block = own_coupling[:, level - 1, :].astype(BF16)
        term = jnp.where(side == 0, fold(mm(both, block)), fold(mt(both, block)))
        down_high[level - 1], down_low[level - 1] = high_low(term)
        terms.append(term)
        if level < 8:
            left, right = halves_of(own_transfer[level - 1])
            path = fold(mt(both, jnp.where(side == 0, left, right)))
    plane = pos >> 5
    handles[early].wait()
    near_node = (plane >> 1) ^ 1
    far_node = (plane >> 2) ^ 1
    two = fold(mm(split(terms[6]), top[near_node]))
    halves = halves_of(fold(mm(split(terms[7]), top[4 + far_node])))
    fours = [fold(mm(split(half), top[2 * far_node + n])) for n, half in enumerate(halves)]
    for n, wide in enumerate([two] + fours):
        high, low = high_low(wide)
        cross_high[n], cross_low[n] = widened(high), widened(low)
    zero = jnp.zeros((64, 64), BF16)
    for out, part in zip((next_high, next_low), high_low(terms[5])):
        out[:64] = paired(part, zero)
        out[64:] = paired(zero, part)
    for handle in handles[early + 1 :]:
        handle.wait()


def widen_kernel(transfer, wide):
    for n in range(15):
        wide[n] = widened(transfer[n])


def plane_kernel(received, wide, message, siblings, nodes):
    tops = [mt(paired(received[2 * n], received[2 * n + 1]), wide[n]) for n in range(8)]
    offset = 0
    while True:
        if len(tops) == 1:
            break
        for n, top in enumerate(tops):
            nodes[offset + n] = top
        offset += len(tops)
        tops = [
            up_packed(tops[2 * n], tops[2 * n + 1], wide[offset + n]) for n in range(len(tops) // 2)
        ]
    root = tops[0].astype(BF16)
    for peer in range(8):
        message[peer] = root
    own = (position() >> 1) & 15
    siblings[0] = received[own ^ 1].astype(F32)
    siblings[1] = nodes[(own >> 1) ^ 1]
    siblings[2] = nodes[8 + ((own >> 2) ^ 1)]
    siblings[3] = nodes[12 + ((own >> 3) ^ 1)]


def add_terms(total, siblings, down_high, down_low, first):
    for n, sibling in enumerate(siblings):
        both = split(sibling)
        total = total + fold(mt(both, down_high[first + n])) + mt(both[:64], down_low[first + n])
    return total


def near_far_kernel(
    near_ids, far_ids, pair, moved, passed, blocks, coupling, sibling, siblings,
    down_high, down_low, near_out, far_out, coef_out, skels,
):
    pos = position()
    odd = pos & 1
    pair_at, moved_at, passed_at = 2 - odd, 3 * odd, 4 - 4 * odd
    coef_out[...] = packed(add_terms(
        jnp.zeros((64, 64), F32), [sibling[...]] + [unpacked(siblings[n]) for n in range(4)],
        down_high, down_low, 0,
    ))
    first_leaf = (pos - 2) * 8
    for source, at, count in ((pair, pair_at, 2), (moved, moved_at, 2), (passed, passed_at, 1)):
        for device in range(count):
            for leaf in range(8):
                lane = 64 * (leaf % 4)
                skels[8 * (at + device) + leaf] = source[device, 8 + leaf // 4, :, lane : lane + 64]
    for g in range(8):
        total = mt(pair[odd, g], blocks[g, 0])
        for k in range(1, 4):
            place = jnp.clip(near_ids[k, g] - first_leaf, 0, 39)
            device, leaf = place >> 3, place & 7
            from_pair, from_moved = device - pair_at, device - moved_at
            cols = jnp.where(
                (from_pair >> 1) == 0, pair[from_pair & 1, leaf],
                jnp.where(
                    (from_moved >> 1) == 0, moved[from_moved & 1, leaf], passed[0, leaf]
                ),
            )
            total = total + mt(cols, blocks[g, k])
        near_out[g] = total
        total = None
        for k in range(8):
            place = jnp.clip(far_ids[g, k] - first_leaf, 0, 39)
            term = mt(skels[place], coupling[g, k])
            total = term if total is None else total + term
        far_out[g] = total


def final_kernel(
    received, next_high, next_low, cross_high, cross_low, leaf_high, leaf_low, coef, near, far, basis,
    out,
):
    own = position() >> 5
    two = ((own >> 1) ^ 1) * 2
    four = ((own >> 2) ^ 1) * 4
    one = received[own ^ 1]
    total = coef[...] + mt(one, next_high[...]) + mt(one, next_low[...])
    for n, first in enumerate((two, four, four + 2)):
        pair = paired(received[first], received[first + 1])
        total = total + mt(pair, cross_high[n]) + mt(pair, cross_low[n])
    total = unpacked(total)
    both = split(total)
    for pair in range(4):
        coefs = fold(mm(both, leaf_high[pair])) + mm(both[:64], leaf_low[pair])
        for side, part in enumerate(halves_of(coefs)):
            g = 2 * pair + side
            half = (part + far[g]).astype(BF16)
            out[g] = (mm(half, basis[g]) + near[g]).astype(BF16)


def call(kernel, ins, outs, in_specs, scratch=(), limit=4, out_spec=VM):
    ins = [
        pltpu.with_memory_space_constraint(x, pltpu.HBM) if spec is HB else x
        for x, spec in zip(ins, in_specs)
    ]
    return pl.pallas_call(
        kernel,
        out_shape=[space(shape, dtype) for shape, dtype, space in outs],
        in_specs=in_specs,
        out_specs=[out_spec] * len(outs),
        scratch_shapes=list(scratch),
        compiler_params=pltpu.CompilerParams(vmem_limit_bytes=limit << 20),
    )(*ins)


def groups_of(bits):
    mask = sum(1 << b for b in bits)
    found = {}
    for device in range(256):
        found.setdefault(device & ~mask, []).append(device)
    return list(found.values())


def exchange(message, bits):
    return lax.all_to_all(message, AXES, 0, 0, axis_index_groups=groups_of(bits))


def swapped(value):
    return lax.ppermute(value, AXES, [(i, i ^ 1) for i in range(lax.axis_size(AXES))])


def outward(value):
    count = lax.axis_size(AXES)
    pairs = [(i, i + 2 - 4 * (i % 2)) for i in range(count)]
    return lax.ppermute(value, AXES, [(i, j) for i, j in pairs if 0 <= j < count])


def local(
    points, basis, near_blocks, near_ids, local_transfer, far_coupling, far_ids,
    upper_transfer, upper_coupling,
):
    near_ids = near_ids.T
    local_transfer = jnp.swapaxes(local_transfer, 1, 2)
    upper_transfer = jnp.swapaxes(upper_transfer, 1, 2)
    upper_coupling = jnp.transpose(upper_coupling, (1, 2, 0))
    halo, root, first, plane = call(
        leaf_up_kernel, (points, basis, local_transfer, upper_transfer),
        [
            ((10, 64, 256), BF16, VMEM), ((64, 64), F32, VMEM), ((2, 64, 64), BF16, VMEM),
            ((15, 64, 128), BF16, VMEM),
        ],
        [HB] * 4,
        [
            pltpu.VMEM((8, 64, 256), BF16), pltpu.VMEM((7, 64, 128), BF16),
            pltpu.VMEM((64, 128), BF16), pltpu.SemaphoreType.DMA((8,)),
        ],
    )
    partner = swapped(root)
    partner_halo = swapped(halo)
    message, sibling = call(
        merge_kernel, (root, partner, first),
        [((16, 32, 128), BF16, HBM), ((64, 64), F32, VMEM)], [VM] * 3,
    )
    received = exchange(message, (1, 2, 3, 4))
    (pair,) = call(
        assemble_kernel, (halo, partner_halo), [((2, 10, 64, 256), BF16, VMEM)],
        [ANY, ANY], [pltpu.SemaphoreType.DMA((2,))],
    )
    moved = outward(pair)
    (wide,) = call(widen_kernel, (plane,), [((15, 128, 256), BF16, VMEM)], [VM])
    message, siblings = call(
        plane_kernel, (received, wide),
        [((8, 32, 128), BF16, HBM), ((4, 32, 128), F32, VMEM)], [VM] * 2,
        [pltpu.VMEM((14, 32, 128), F32)],
    )
    received = exchange(message, (5, 6, 7))
    odd = lax.axis_index("cy") & 1
    passed = swapped(lax.dynamic_slice_in_dim(moved, 1 - odd, 1, 0))
    (
        next_high, next_low, cross_high, cross_low, down_high, down_low, leaf_high, leaf_low,
        basis, near_blocks, far_coupling,
    ) = call(
        weights_kernel,
        (upper_transfer, upper_coupling, local_transfer, basis, near_blocks, far_coupling),
        [((128, 128), BF16, VMEM)] * 2 + [((3, 128, 256), BF16, VMEM)] * 2
        + [((8, 64, 64), BF16, VMEM)] * 2
        + [((4, 64, 128), BF16, VMEM)] * 2
        + [((8, 64, 256), BF16, VMEM), ((8, 4, 256, 256), BF16, VMEM), ((8, 8, 64, 64), BF16, VMEM)],
        [HB] * 6,
        [
            pltpu.VMEM((6, 64, 128), BF16), pltpu.VMEM((8, 64, 128), BF16),
            pltpu.VMEM((64, 8, 64), F32),
            pltpu.VMEM((64, 64, 255), BF16), pltpu.VMEM((7, 64, 128), BF16),
            pltpu.SemaphoreType.DMA((14,)),
        ],
        limit=8,
    )
    near, far, coef = call(
        near_far_kernel,
        (near_ids, far_ids, pair, moved, passed, near_blocks, far_coupling, sibling, siblings,
         down_high, down_low),
        [((8, 64, 256), F32, VMEM), ((8, 64, 64), F32, VMEM), ((32, 128), F32, VMEM)],
        [SM, SM] + [VM] * 9,
        [pltpu.VMEM((40, 64, 64), BF16)],
    )
    (out,) = call(
        final_kernel,
        (received, next_high, next_low, cross_high, cross_low, leaf_high, leaf_low, coef, near, far,
         basis),
        [((8, 64, 256), BF16, HBM)], [VM] * 11,
    )
    return out


def solution(mesh):
    return jax.shard_map(
        local,
        mesh=mesh,
        in_specs=(
            P(AXES, None, None),
            P(AXES, None, None),
            P(AXES, None, None, None),
            P(AXES, None),
            P(AXES, None, None),
            P(AXES, None, None, None),
            P(AXES, None),
            P(),
            P(),
        ),
        out_specs=P(AXES, None, None),
        check_vma=False,
    )
```
